32 devices in a mesh: row: 2 (over x), col: 4 (over y, core), grid: 4 (over z).
Axes of the slice: x: 2, y: 2, z: 4, core: 2. Of those that a mesh axis runs over, the one named last changes fastest.
Arguments:
- snapshots: bfloat16 [16384, 1024], P(('row', 'col', 'grid')), may hold values from -6 to 6
- jitter_code: int32 [16384], replicated, may hold values from 0 to 63
- slab_start: int32 [4], P('grid'), may hold values from 0 to 127
- gamma: float32 [2048], P('grid'), may hold values from 0.1 to 10
- noise_var: float32 [1], replicated, may hold values from 0.3 to 1.5
Outputs:
- steered: float32 [16384, 2048], P(('row', 'col'), 'grid')
- gamma_new: float32 [2048], P('grid')
The draws below stay inside these ranges and needn't reach their ends.
All inputs are finite; a program needn't handle non-finite values.
Results may differ from the reference program's by a relative error of at most 0.0003.
Values may be sent and summed in bfloat16 or wider, within the bound.
A program may use at most 64 MiB of HBM per device.

```python
import math
import jax
import jax.numpy as jnp
from jax import lax

M = 16384
SNAP = 1024
SLAB = 512
GRID = 65536
POINTS = 2048
N_GRID = 4


def set_ends(drawn, rng, least, largest):
    longest = drawn.shape.index(max(drawn.shape))
    spots = []
    for shift in (0, 1):
        where = [jax.random.randint(jax.random.fold_in(rng, axis), (), 0, length) for axis, length in enumerate(drawn.shape)]
        where[longest] = (where[longest] + shift) % drawn.shape[longest]
        spots.append(tuple(where))
    return drawn.at[spots[0]].set(least).at[spots[1]].set(largest)


def level_of(stream_key, dims, shards, least, top_value):
    factor_of, own = 1.0, jax.random.fold_in(stream_key, 6)
    for dim, shards_of in shards:
        heights = jnp.exp(jax.random.uniform(jax.random.fold_in(own, dim), (shards_of,), jnp.float32, least / len(shards), top_value / len(shards)))
        factor_of = factor_of * jnp.repeat(heights, dims[dim] // shards_of).reshape([-1 if axis == dim else 1 for axis in range(len(dims))])
    return factor_of


def bell_draw(key, shape, width, most, cuts=(), kind=jnp.bfloat16):
    gain = level_of(key, shape, cuts, -0.22, 0.18) if cuts else 1.0
    array = jax.random.normal(key, shape, jnp.float32) * width * gain
    return jnp.minimum(jnp.maximum(array, -most), most).astype(kind)


def setup_inputs(seed: int = 0) -> dict:
    keys = jax.random.split(jax.random.key(seed), 6)
    snapshots = bell_draw(keys[0], (M, SNAP), 1.0, 6.0, ((0, 32),))
    jitter_code = set_ends(jax.random.randint(keys[1], (M,), 0, 64), jax.random.fold_in(keys[1], 1), 0, 63).astype(jnp.int32)
    slab_start = set_ends(jax.random.randint(keys[2], (N_GRID,), 0, GRID // SLAB), jax.random.fold_in(keys[2], 1), 0, (GRID // SLAB) - 1).astype(jnp.int32)
    gamma = jnp.clip(jnp.exp(math.log(10.0) - 4.6051702 * jax.random.uniform(keys[3], (POINTS,), jnp.float32) ** level_of(keys[3], (POINTS,), ((0, 4),), -0.2, 0.2)), 0.1, 10.0)
    noise_var = jnp.clip(jax.random.uniform(keys[4], (1,), jnp.float32, 0.3, 1.5), 0.3, 1.5)
    return dict(snapshots=snapshots, jitter_code=jitter_code, slab_start=slab_start, gamma=gamma, noise_var=noise_var)


def steer(sensor, codes, points):
    pos = (64 * sensor + codes + 32).astype(jnp.int32)[:, None]
    low = (points % 256).astype(jnp.int32)[None, :]
    high = (points // 256).astype(jnp.int32)[None, :]
    modulus = 64 * GRID
    first = (pos * low) % modulus
    second = ((pos * high) % (modulus // 256)) * 256
    wound = (first + second) % modulus
    turns = wound.astype(jnp.float32) / modulus - (pos % 128).astype(jnp.float32) / 128.0
    return jnp.cos(2.0 * jnp.pi * turns)


def reference(snapshots, jitter_code, slab_start, gamma, noise_var):
    sensors = jnp.arange(M, dtype=jnp.int32)
    stride = GRID // SLAB
    points = (slab_start[:, None] + stride * jnp.arange(SLAB, dtype=jnp.int32)[None, :]).reshape(-1).astype(jnp.int32)
    steering = steer(sensors, jitter_code, points)
    data = snapshots.astype(jnp.float32)
    projected = jnp.dot(data.T, steering, precision=lax.Precision.HIGHEST)
    steered = jnp.dot(data, projected, precision=lax.Precision.HIGHEST) / SNAP
    forms = jnp.sum(steering * steered, axis=0)
    norms = jnp.sum(steering * steering, axis=0)
    gamma_new = gamma * forms / (norms * (gamma + noise_var[0]))
    return steered, gamma_new
```

```python
import functools

import jax
import jax.numpy as jnp
from jax import lax
from jax.experimental import pallas as pl
from jax.experimental.pallas import tpu as pltpu
from jax.sharding import PartitionSpec as P

GRID = 65536
WIDTH = 256
LANES = 128
F32 = jnp.float32
BF16 = jnp.bfloat16
MESH = pl.DeviceIdType.MESH


def sine(turns):
    z = turns * turns
    p = F32(39.53581371)
    p = p * z + F32(-76.54965682)
    p = p * z + F32(81.60099819)
    p = p * z + F32(-41.34165493)
    p = p * z + F32(6.28318516)
    return p * turns


def split(x):
    hi = x.astype(BF16)
    return hi, (x - hi.astype(F32)).astype(BF16)


def fold(x):
    n = x.shape[1]
    if n % LANES:
        total = jnp.sum(x, axis=1, keepdims=True)
        lane = lax.broadcasted_iota(jnp.int32, (x.shape[0], LANES), 1)
        return jnp.where(lane == 0, total, 0.0)
    return sum(x[:, a : a + LANES] for a in range(0, n, LANES))


def helped_blocks(n_grid, n_block):
    return list(range(n_block - n_block // 2, n_block)) if n_grid >= 4 else []


class Plan:
    def __init__(self, n_row, n_col, points):
        self.core = points // 2
        rest = [d for d in ((n_col // 2, "y"), (n_row, "row")) if d[0] > 1]
        total = 1
        for n, _ in rest:
            total *= n
        both = len(rest) == 2 and (self.core // total) % 16 == 0
        self.paths = [rest, rest[::-1]] if both else [rest]
        self.length = self.core // len(self.paths)
        self.shard = self.length // total
        self.depth = len(rest)
        at, event = 2 * self.core, 1
        self.land, self.sums, self.events, self.sizes = [], [], [], []
        for dims in self.paths:
            land, sums, events, sizes = [], [], [], []
            size = self.length
            for n, _ in dims:
                size //= n
                land.append(at)
                at += (n - 1) * size
                sums.append(at)
                at += size
                events.append(event)
                event += n - 1
                sizes.append(size)
            self.land.append(land)
            self.sums.append(sums)
            self.events.append(events)
            self.sizes.append(sizes)
        self.rows = at
        self.n_event = event


def kernel(
    sizes, start_ref, jitter_ref, snaps_ref, partly_ref, last_ref, hi_ref, lo_ref, forms_ref, norms_ref,
    held, steer_hi, steer_lo, far_hi, far_lo, parts, far_part, full, out, proj_hi, proj_lo, forms,
    part_norm, norms, work, work_norm, far_sum, far_in, jitter, positions, start_out, start_in,
    load_sem, misc_sem, z_send, z_recv, p_send, p_recv, f_send, f_recv, s_send, s_recv, o_sem,
):
    n_row, n_col, n_grid, stride = sizes
    n_block, _, rows, width = held.shape
    points = parts.shape[1]
    snap = n_block * width
    plan = Plan(n_row, n_col, points)
    helped = helped_blocks(n_grid, n_block)
    row, col, z = (lax.axis_index(a) for a in ("row", "col", "grid"))
    place = {"core": col % 2, "y": col // 2, "row": row}
    is_end = jnp.logical_or(z == 0, z == n_grid - 1)
    not_end = jnp.logical_not(is_end)
    helps = jnp.logical_or(z == 1, z == n_grid - 2)
    if not helped:
        is_end, not_end = None, None
    end_of = jnp.where(z == 1, 0, n_grid - 1)
    helper_of = jnp.where(z == 0, 1, n_grid - 2)

    def when(ok, action):
        if ok is None:
            action()
        else:
            pl.when(ok)(action)

    def peer(kind, other):
        if kind == "row":
            return (other, col, z)
        if kind == "core":
            return (row, (col // 2) * 2 + other, z)
        return (row, other * 2 + col % 2, z)

    def others(n, kind):
        return [lax.rem(place[kind] + p, n) for p in range(1, n)]

    peers = [peer("core", 1 - place["core"])]
    for n, kind in plan.paths[0]:
        peers += [peer(kind, other) for other in others(n, kind)]
    up, down = (row, col, z + 1), (row, col, z - 1)

    loads = [
        pltpu.make_async_copy(
            snaps_ref.at[:, pl.ds(k * width, width)], held.at[k, z], load_sem.at[k]
        )
        for k in range(n_block)
    ]
    for load in loads:
        load.start()
    codes = pltpu.make_async_copy(jitter_ref.at[row * n_col + col], jitter, misc_sem.at[0])
    codes.start()
    start_out[...] = jnp.full(start_out.shape, start_ref[0], jnp.int32)
    barrier = pltpu.get_barrier_semaphore()
    for device in peers:
        pl.semaphore_signal(barrier, inc=1, device_id=device, device_id_type=MESH)

    @pl.when(z + 1 < n_grid)
    def _():
        pl.semaphore_signal(barrier, inc=1, device_id=up, device_id_type=MESH)

    @pl.when(z > 0)
    def _():
        pl.semaphore_signal(barrier, inc=1, device_id=down, device_id_type=MESH)

    beside = jnp.minimum(z, 1) + jnp.minimum(n_grid - 1 - z, 1)
    pl.semaphore_wait(barrier, len(peers) + beside)


    def hop(k, s, direction, origin):
        return pltpu.make_async_remote_copy(
            src_ref=held.at[k, origin],
            dst_ref=held.at[k, origin],
            send_sem=z_send.at[direction, k, s],
            recv_sem=z_recv.at[direction, k, s],
            device_id=up if direction == 0 else down,
            device_id_type=MESH,
        )

    def can_send(s, direction):
        if direction == 0:
            return jnp.logical_and(z + 1 < n_grid, z - s >= 0), z - s
        return jnp.logical_and(z > 0, z + s < n_grid), z + s

    def can_receive(s, direction):
        if direction == 0:
            return z - s - 1 >= 0, z - s - 1
        return z + s + 1 < n_grid, z + s + 1

    def send(k, s, to_end=None):
        for direction in (0, 1):
            ok, origin = can_send(s, direction)
            if to_end is not None:
                last = z + 1 == n_grid - 1 if direction == 0 else z - 1 == 0
                ok = jnp.logical_and(ok, last if to_end else jnp.logical_not(last))

            @pl.when(ok)
            def _():
                hop(k, s, direction, origin).start()

    def receive(k, s, only=None):
        for direction in (0, 1):
            ok, origin = can_receive(s, direction)
            if only is not None:
                ok = jnp.logical_and(ok, only)

            @pl.when(ok)
            def _():
                hop(k, s, direction, origin).wait_recv()

    def drain(k, s):
        for direction in (0, 1):
            ok, origin = can_send(s, direction)

            @pl.when(ok)
            def _():
                hop(k, s, direction, origin).wait_send()

    def start_copy(device):
        return pltpu.make_async_remote_copy(
            src_ref=start_out,
            dst_ref=start_in,
            send_sem=s_send.at[0],
            recv_sem=s_recv.at[0],
            device_id=device,
            device_id_type=MESH,
        )

    if helped:
        pl.when(is_end)(lambda: start_copy((row, col, helper_of)).start())
    for k in range(n_block):
        loads[k].wait()
        send(k, 0)


    def aligned(index):
        return pl.multiple_of(index, 8)

    class Sum:
        def __init__(self, index, source, target, area, compact=False):
            self.index, self.source, self.target, self.area = index, source, target, area
            self.compact = compact

        def copy(self, src, dst, event, device):
            return pltpu.make_async_remote_copy(
                src_ref=src,
                dst_ref=dst,
                send_sem=p_send.at[self.index, event],
                recv_sem=p_recv.at[self.index, event],
                device_id=device,
                device_id_type=MESH,
            )

        def core_copy(self):
            other = 1 - place["core"]
            return self.copy(
                self.source.at[pl.ds(aligned(other * plan.core), plan.core), :],
                self.area.at[pl.ds(0, plan.core), :],
                0,
                peer("core", other),
            )

        def core_add(self):
            self.core_copy().wait()
            mine = pl.ds(aligned(place["core"] * plan.core), plan.core)
            self.area[pl.ds(plan.core, plan.core), :] = (
                self.source[mine, :] + self.area[pl.ds(0, plan.core), :]
            )

        def step_copies(self, j):
            copies = []
            for path, dims in enumerate(plan.paths):
                n, kind = dims[j]
                size = plan.sizes[path][j]
                base = plan.core + path * plan.length if j == 0 else plan.sums[path][j - 1]
                for p, other in enumerate(others(n, kind)):
                    copies.append(
                        self.copy(
                            self.area.at[pl.ds(aligned(base + other * size), size), :],
                            self.area.at[pl.ds(plan.land[path][j] + p * size, size), :],
                            plan.events[path][j] + p,
                            peer(kind, other),
                        )
                    )
            return copies

        def offset(self, path, j):
            at = place["core"] * plan.core + path * plan.length
            for (_, kind), size in zip(plan.paths[path][:j], plan.sizes[path][:j]):
                at = at + place[kind] * size
            return at

        def step_add(self, j):
            for copy in self.step_copies(j):
                copy.wait()
            for path, dims in enumerate(plan.paths):
                n, kind = dims[j]
                size = plan.sizes[path][j]
                base = plan.core + path * plan.length if j == 0 else plan.sums[path][j - 1]
                total = self.area[pl.ds(aligned(base + place[kind] * size), size), :]
                for p in range(n - 1):
                    total = total + self.area[pl.ds(plan.land[path][j] + p * size, size), :]
                if j + 1 < len(dims):
                    self.area[pl.ds(plan.sums[path][j], size), :] = total
                elif self.compact:
                    self.target[pl.ds(path * plan.shard, size), :] = total
                else:
                    self.target[pl.ds(aligned(self.offset(path, j + 1)), size), :] = total

        def step_back(self, j):
            copies = []
            for path, dims in enumerate(plan.paths):
                n, kind = dims[j]
                size = plan.sizes[path][j]
                mine = pl.ds(aligned(self.offset(path, j + 1)), size)
                for p, other in enumerate(others(n, kind)):
                    copies.append(
                        self.copy(
                            self.target.at[mine, :],
                            self.target.at[mine, :],
                            plan.n_event + plan.events[path][j] + p,
                            peer(kind, other),
                        )
                    )
            return copies

        def core_back(self):
            mine = pl.ds(aligned(place["core"] * plan.core), plan.core)
            return self.copy(
                self.target.at[mine, :],
                self.target.at[mine, :],
                plan.n_event,
                peer("core", 1 - place["core"]),
            )

        def scatter(self, ok=None):
            when(ok, lambda: self.core_copy().start())
            yield
            when(ok, self.core_add)
            for j in range(plan.depth):

                def go(j=j):
                    for copy in self.step_copies(j):
                        copy.start()

                when(ok, go)
                yield
                when(ok, functools.partial(self.step_add, j))

        def gather(self):
            for j in reversed(range(plan.depth)):
                for copy in self.step_back(j):
                    copy.start()
                yield
                for copy in self.step_back(j):
                    copy.wait()
            self.core_back().start()
            yield
            self.core_back().wait()

    active, summed, finished = [], [], []

    def tick(count=1):
        for _ in range(count):
            for steps in list(active):
                if next(steps, "end") == "end":
                    active.remove(steps)

    def spawn(steps):
        active.append(steps)
        next(steps)


    def find_positions():
        base = (row * n_col + col) * n_grid * rows
        for g in range(n_grid):
            sensor = base + g * rows + lax.broadcasted_iota(jnp.int32, (1, rows), 1)
            positions[g] = 64 * sensor + jitter[g] + 32

    def steer(first_point, count, group, hi_to, lo_to, norm):
        tile = min(32, points)
        tiles = points // tile

        def body(i, carry):
            j, first = i // tiles, pl.multiple_of((i % tiles) * tile, tile)
            pos = positions[group(j)]
            point = first_point() + stride * (
                first + lax.broadcasted_iota(jnp.int32, (tile, 1), 0)
            )
            phase = (point * pos - ((pos & 127) << 15)) << 10
            turns = phase.astype(F32) * F32(2.0**-32)
            value = sine(0.25 - jnp.abs(turns))
            hi, lo = split(value)
            hi_to[j, pl.ds(first, tile), :] = hi
            lo_to[j, pl.ds(first, tile), :] = lo
            if norm:
                part_norm[pl.ds(first, tile), :] += fold(value * value)
            return carry

        lax.fori_loop(0, count * tiles, body, 0)

    def far_group(j):
        return jnp.where(z == 1, z + 1 + j, j)

    def dots(hi, lo, block):
        value = jnp.dot(hi, block, preferred_element_type=F32)
        return value + jnp.dot(lo, block, preferred_element_type=F32)

    def project(k, origin, fresh=False):
        value = dots(steer_hi[origin], steer_lo[origin], held[k, origin])
        if fresh:
            parts[k] = value
        else:
            parts[k] += value

    def project_arrived(k, s, only=None):
        for direction in (0, 1):
            ok, origin = can_receive(s, direction)
            if only is not None:
                ok = jnp.logical_and(ok, only)

            @pl.when(ok)
            def _():
                project(k, origin)

    def project_far(k):
        i = helped.index(k)
        total = None
        for j in range(far_hi.shape[0]):
            value = dots(far_hi[j], far_lo[j], held[k, far_group(j)])
            total = value if total is None else total + value
        far_part[i] = total

    def far_copy(i):
        return pltpu.make_async_remote_copy(
            src_ref=far_sum.at[i],
            dst_ref=far_in.at[i],
            send_sem=f_send.at[i],
            recv_sem=f_recv.at[i],
            device_id=(row, col, end_of),
            device_id_type=MESH,
        )

    sums = [Sum(k, parts.at[k], full.at[k], work.at[k]) for k in range(n_block)]
    norm_sum = Sum(n_block, part_norm, norms, work_norm)
    far_sums = [
        Sum(n_block + 1 + i, far_part.at[i], far_sum.at[i], work.at[n_block + i], compact=True)
        for i in range(len(helped))
    ]

    def add_far(k):
        i = helped.index(k)
        far_copy(i).wait_recv()
        for path in range(len(plan.paths)):
            spot = pl.ds(aligned(sums[k].offset(path, plan.depth)), plan.shard)
            full[k, spot, :] += far_in[i, pl.ds(path * plan.shard, plan.shard), :]

    def reduce(k):
        yield from sums[k].scatter(not_end if k in helped else None)
        if k in helped:
            for other in range(helped[0]):
                if other in summed and other not in finished:
                    finish_block(other, is_end)
                    finished.append(other)
            when(is_end, functools.partial(add_far, k))
        yield from sums[k].gather()
        summed.append(k)

    def reduce_far(k):
        i = helped.index(k)
        yield from far_sums[i].scatter(helps)
        when(helps, lambda: far_copy(i).start())

    def reduce_norm():
        yield from norm_sum.scatter()
        yield from norm_sum.gather()

    def prepare(k):
        value = full[k]
        square = fold(value * value)
        forms[...] = square if k == 0 else forms[...] + square
        hi, lo = split(value / snap)
        proj_hi[k] = hi
        proj_lo[k] = lo

    def apply(k):
        dims_nt = (((1,), (1,)), ((), ()))

        def body(g, carry):
            block = held[k, g]
            added = lax.dot_general(block, proj_hi[k], dims_nt, preferred_element_type=F32)
            added += lax.dot_general(block, proj_lo[k], dims_nt, preferred_element_type=F32)
            spot = pl.ds(pl.multiple_of(g * rows, rows), rows)
            out[spot, :] = added if k == 0 else out[spot, :] + added
            return carry

        lax.fori_loop(0, n_grid, body, 0)

    def finish_block(k, only=None):
        def go():
            prepare(k)
            if k + 1 < n_block:
                apply(k)

        when(only, go)

    codes.wait()
    find_positions()
    part_norm[...] = jnp.zeros_like(part_norm)
    steer(lambda: start_ref[0], n_grid, lambda j: j, steer_hi, steer_lo, True)
    spawn(reduce_norm())
    for k in range(n_block):
        project(k, z, fresh=True)
    tick()
    if helped:

        @pl.when(helps)
        def _():
            start_copy((row, col, end_of)).wait_recv()
            steer(lambda: start_in[0:1, 0:1], n_grid - 2, far_group, far_hi, far_lo, False)

    tick()
    for k in range(n_block):
        receive(k, 0)
        if n_grid > 2:
            send(k, 1, to_end=False)
            if k not in helped:
                send(k, 1, to_end=True)
        project_arrived(k, 0)
        tick()
    early = [sums[k].scatter(is_end) for k in helped]
    for steps in early:
        next(steps)
    for _ in range(plan.depth + 1):
        for steps in early:
            next(steps, None)
    for k in range(n_block):
        if k in helped:
            continue
        for s in range(1, n_grid - 1):
            receive(k, s)
            if s + 1 < n_grid - 1:
                send(k, s + 1)
            project_arrived(k, s)
        spawn(reduce(k))
        tick(2)
    waiting = [(k, s) for k in helped for s in range(1, n_grid - 1)]
    for k in helped:
        for s in range(1, n_grid - 1):
            receive(k, s, not_end)
            if s + 1 < n_grid - 1:
                send(k, s + 1, to_end=False)
        send(*waiting.pop(0), to_end=True)
        for s in range(1, n_grid - 1):
            project_arrived(k, s, not_end)
        pl.when(helps)(functools.partial(project_far, k))
        spawn(reduce_far(k))
        spawn(reduce(k))
        tick(2)
    tick(2)
    for k, s in waiting:
        send(k, s, to_end=True)
    while active:
        tick()
    for k in range(n_block):
        if k in finished:
            finish_block(k, not_end)
            continue
        if k in helped and k + 1 < n_block:
            for s in range(1, n_grid - 1):
                receive(k, s, is_end)
        finish_block(k)

    outs = [
        pltpu.make_async_copy(src, dst, o_sem.at[i])
        for i, (src, dst) in enumerate(
            (
                (out, partly_ref),
                (proj_hi.at[n_block - 1], hi_ref),
                (proj_lo.at[n_block - 1], lo_ref),
                (forms, forms_ref),
                (norms, norms_ref),
                (held.at[n_block - 1], last_ref),
            )
        )
    ]
    for copy in outs[:-1]:
        copy.start()
    if helped:
        for s in range(1, n_grid - 1):
            receive(n_block - 1, s, is_end)
    outs[-1].start()
    for k in range(n_block):
        for s in range(n_grid - 1):
            drain(k, s)
    if helped:
        pl.when(is_end)(lambda: start_copy((row, col, helper_of)).wait_send())

        @pl.when(helps)
        def _():
            for i in range(len(helped)):
                far_copy(i).wait_send()

    for copy in outs:
        copy.wait()


def finish(snap, partly_ref, held_ref, hi_ref, lo_ref, forms_ref, norms_ref, gamma_ref, noise_ref, out_ref, new_ref):
    dims_nt = (((1,), (1,)), ((), ()))
    block = held_ref[...]
    added = lax.dot_general(block, hi_ref[...], dims_nt, preferred_element_type=F32)
    added += lax.dot_general(block, lo_ref[...], dims_nt, preferred_element_type=F32)
    out_ref[...] = partly_ref[...] + added

    @pl.when(pl.program_id(0) == 0)
    def _():
        form = jnp.sum(forms_ref[...].T, axis=0, keepdims=True) / snap
        norm = jnp.sum(norms_ref[...].T, axis=0, keepdims=True)
        gamma = gamma_ref[...]
        new_ref[...] = gamma * form / (norm * (gamma + noise_ref[0]))


def on_device(snapshots, jitter_code, slab_start, gamma, noise_var):
    n_row, n_col, n_grid = (lax.axis_size(a) for a in ("row", "col", "grid"))
    rows, snap = snapshots.shape
    group_rows = rows * n_grid
    points = gamma.shape[0]
    width = min(WIDTH, snap)
    n_block = snap // width
    plan = Plan(n_row, n_col, points)
    n_help = len(helped_blocks(n_grid, n_block))
    n_far = max(n_help, 1)
    shard = len(plan.paths) * plan.shard
    vmem = pl.BlockSpec(memory_space=pltpu.VMEM)
    any_space = pl.BlockSpec(memory_space=pl.ANY)
    n_sum = n_block + 1 + n_far
    dma = pltpu.SemaphoreType.DMA
    partly, last, hi, lo, forms, norms = pl.pallas_call(
        functools.partial(kernel, (n_row, n_col, n_grid, GRID // points)),
        out_shape=(
            jax.ShapeDtypeStruct((group_rows, points), F32),
            jax.ShapeDtypeStruct((n_grid, rows, width), BF16),
            jax.ShapeDtypeStruct((points, width), BF16),
            jax.ShapeDtypeStruct((points, width), BF16),
            jax.ShapeDtypeStruct((points, LANES), F32),
            jax.ShapeDtypeStruct((points, LANES), F32),
        ),
        in_specs=[pl.BlockSpec(memory_space=pltpu.SMEM), any_space, any_space],
        out_specs=(any_space,) * 6,
        scratch_shapes=[
            pltpu.VMEM((n_block, n_grid, rows, width), BF16),
            pltpu.VMEM((n_grid, points, rows), BF16),
            pltpu.VMEM((n_grid, points, rows), BF16),
            pltpu.VMEM((max(n_grid - 2, 1), points, rows), BF16),
            pltpu.VMEM((max(n_grid - 2, 1), points, rows), BF16),
            pltpu.VMEM((n_block, points, width), F32),
            pltpu.VMEM((n_far, points, width), F32),
            pltpu.VMEM((n_block, points, width), F32),
            pltpu.VMEM((group_rows, points), F32),
            pltpu.VMEM((n_block, points, width), BF16),
            pltpu.VMEM((n_block, points, width), BF16),
            pltpu.VMEM((points, LANES), F32),
            pltpu.VMEM((points, LANES), F32),
            pltpu.VMEM((points, LANES), F32),
            pltpu.VMEM((n_block + n_far, plan.rows, width), F32),
            pltpu.VMEM((plan.rows, LANES), F32),
            pltpu.VMEM((n_far, shard, width), F32),
            pltpu.VMEM((n_far, shard, width), F32),
            pltpu.VMEM((n_grid, 1, rows), jnp.int32),
            pltpu.VMEM((n_grid, 1, rows), jnp.int32),
            pltpu.VMEM((8, LANES), jnp.int32),
            pltpu.VMEM((8, LANES), jnp.int32),
            dma((n_block,)),
            dma((1,)),
            dma((2, n_block, n_grid - 1)),
            dma((2, n_block, n_grid - 1)),
            dma((n_sum, 2 * plan.n_event)),
            dma((n_sum, 2 * plan.n_event)),
            dma((n_far,)),
            dma((n_far,)),
            dma((1,)),
            dma((1,)),
            dma((6,)),
        ],
        compiler_params=pltpu.CompilerParams(
            collective_id=0, has_side_effects=True, vmem_limit_bytes=48 << 20
        ),
    )(slab_start, jitter_code.reshape(n_row * n_col, n_grid, 1, rows), snapshots)
    tile = min(256, group_rows)

    def whole(*shape):
        return pl.BlockSpec(shape, lambda i: (0, 0))

    def tall(columns):
        return pl.BlockSpec((tile, columns), lambda i: (i, 0))

    steered, gamma_new = pl.pallas_call(
        functools.partial(finish, snap),
        grid=(group_rows // tile,),
        out_shape=(
            jax.ShapeDtypeStruct((group_rows, points), F32),
            jax.ShapeDtypeStruct((1, points), F32),
        ),
        in_specs=[
            tall(points), tall(width), whole(points, width), whole(points, width),
            whole(points, LANES), whole(points, LANES), whole(1, points),
            pl.BlockSpec(memory_space=pltpu.SMEM),
        ],
        out_specs=(tall(points), whole(1, points)),
        compiler_params=pltpu.CompilerParams(vmem_limit_bytes=12 << 20),
    )(
        partly, last.reshape(group_rows, width), hi, lo, forms, norms,
        gamma.reshape(1, points), noise_var,
    )
    return (steered, gamma_new.reshape(points))


def solution(mesh):
    in_specs = (P(("row", "col", "grid"), None), P(), P("grid"), P("grid"), P())
    out_specs = (P(("row", "col"), "grid"), P("grid"))
    return jax.shard_map(
        on_device, mesh=mesh, in_specs=in_specs, out_specs=out_specs, check_vma=False
    )
```

```python
import functools

import jax
import jax.numpy as jnp
from jax import lax
from jax.experimental import pallas as pl
from jax.experimental.pallas import tpu as pltpu
from jax.sharding import PartitionSpec as P

GRID = 65536
WIDTH = 256
LANES = 128
F32 = jnp.float32
BF16 = jnp.bfloat16
MESH = pl.DeviceIdType.MESH


def sine(turns):
    z = turns * turns
    p = F32(39.53581371)
    p = p * z + F32(-76.54965682)
    p = p * z + F32(81.60099819)
    p = p * z + F32(-41.34165493)
    p = p * z + F32(6.28318516)
    return p * turns


def split(x):
    hi = x.astype(BF16)
    return hi, (x - hi.astype(F32)).astype(BF16)


def fold(x):
    n = x.shape[1]
    if n % LANES:
        total = jnp.sum(x, axis=1, keepdims=True)
        lane = lax.broadcasted_iota(jnp.int32, (x.shape[0], LANES), 1)
        return jnp.where(lane == 0, total, 0.0)
    return sum(x[:, a : a + LANES] for a in range(0, n, LANES))


def helped_blocks(n_grid, n_block):
    return list(range(n_block - n_block // 2, n_block)) if n_grid >= 4 else []


class Plan:
    def __init__(self, n_row, n_col, points):
        self.core = points // 2
        rest = [d for d in ((n_col // 2, "y"), (n_row, "row")) if d[0] > 1]
        total = 1
        for n, _ in rest:
            total *= n
        both = len(rest) == 2 and (self.core // total) % 16 == 0
        self.paths = [rest, rest[::-1]] if both else [rest]
        self.length = self.core // len(self.paths)
        self.shard = self.length // total
        self.depth = len(rest)
        at, event = 2 * self.core, 1
        self.land, self.sums, self.events, self.sizes = [], [], [], []
        for dims in self.paths:
            land, sums, events, sizes = [], [], [], []
            size = self.length
            for n, _ in dims:
                size //= n
                land.append(at)
                at += (n - 1) * size
                sums.append(at)
                at += size
                events.append(event)
                event += n - 1
                sizes.append(size)
            self.land.append(land)
            self.sums.append(sums)
            self.events.append(events)
            self.sizes.append(sizes)
        self.rows = at
        self.n_event = event


def kernel(
    sizes, start_ref, jitter_ref, snaps_ref, partly_ref, last_ref, hi_ref, lo_ref, forms_ref, norms_ref,
    held, steer_hi, steer_lo, far_hi, far_lo, parts, far_part, full, out, proj_hi, proj_lo, forms,
    part_norm, norms, work, work_norm, far_sum, far_in, jitter, positions, start_out, start_in,
    load_sem, misc_sem, z_send, z_recv, p_send, p_recv, f_send, f_recv, s_send, s_recv, o_sem,
):
    n_row, n_col, n_grid, stride = sizes
    n_block, _, rows, width = held.shape
    points = parts.shape[1]
    snap = n_block * width
    plan = Plan(n_row, n_col, points)
    helped = helped_blocks(n_grid, n_block)
    row, col, z = (lax.axis_index(a) for a in ("row", "col", "grid"))
    place = {"core": col % 2, "y": col // 2, "row": row}
    is_end = jnp.logical_or(z == 0, z == n_grid - 1)
    not_end = jnp.logical_not(is_end)
    helps = jnp.logical_or(z == 1, z == n_grid - 2)
    if not helped:
        is_end, not_end = None, None
    end_of = jnp.where(z == 1, 0, n_grid - 1)
    helper_of = jnp.where(z == 0, 1, n_grid - 2)

    def when(ok, action):
        if ok is None:
            action()
        else:
            pl.when(ok)(action)

    def peer(kind, other):
        if kind == "row":
            return (other, col, z)
        if kind == "core":
            return (row, (col // 2) * 2 + other, z)
        return (row, other * 2 + col % 2, z)

    def others(n, kind):
        return [lax.rem(place[kind] + p, n) for p in range(1, n)]

    peers = [peer("core", 1 - place["core"])]
    for n, kind in plan.paths[0]:
        peers += [peer(kind, other) for other in others(n, kind)]
    up, down = (row, col, z + 1), (row, col, z - 1)

    loads = [
        pltpu.make_async_copy(
            snaps_ref.at[:, pl.ds(k * width, width)], held.at[k, z], load_sem.at[k]
        )
        for k in range(n_block)
    ]
    for load in loads:
        load.start()
    codes = pltpu.make_async_copy(jitter_ref.at[row * n_col + col], jitter, misc_sem.at[0])
    codes.start()
    start_out[...] = jnp.full(start_out.shape, start_ref[0], jnp.int32)
    barrier = pltpu.get_barrier_semaphore()
    for device in peers:
        pl.semaphore_signal(barrier, inc=1, device_id=device, device_id_type=MESH)

    @pl.when(z + 1 < n_grid)
    def _():
        pl.semaphore_signal(barrier, inc=1, device_id=up, device_id_type=MESH)

    @pl.when(z > 0)
    def _():
        pl.semaphore_signal(barrier, inc=1, device_id=down, device_id_type=MESH)

    beside = jnp.minimum(z, 1) + jnp.minimum(n_grid - 1 - z, 1)
    pl.semaphore_wait(barrier, len(peers) + beside)


    def hop(k, s, direction, origin):
        return pltpu.make_async_remote_copy(
            src_ref=held.at[k, origin],
            dst_ref=held.at[k, origin],
            send_sem=z_send.at[direction, k, s],
            recv_sem=z_recv.at[direction, k, s],
            device_id=up if direction == 0 else down,
            device_id_type=MESH,
        )

    def can_send(s, direction):
        if direction == 0:
            return jnp.logical_and(z + 1 < n_grid, z - s >= 0), z - s
        return jnp.logical_and(z > 0, z + s < n_grid), z + s

    def can_receive(s, direction):
        if direction == 0:
            return z - s - 1 >= 0, z - s - 1
        return z + s + 1 < n_grid, z + s + 1

    def send(k, s, to_end=None):
        for direction in (0, 1):
            ok, origin = can_send(s, direction)
            if to_end is not None:
                last = z + 1 == n_grid - 1 if direction == 0 else z - 1 == 0
                ok = jnp.logical_and(ok, last if to_end else jnp.logical_not(last))

            @pl.when(ok)
            def _():
                hop(k, s, direction, origin).start()

    def receive(k, s, only=None):
        for direction in (0, 1):
            ok, origin = can_receive(s, direction)
            if only is not None:
                ok = jnp.logical_and(ok, only)

            @pl.when(ok)
            def _():
                hop(k, s, direction, origin).wait_recv()

    def drain(k, s):
        for direction in (0, 1):
            ok, origin = can_send(s, direction)

            @pl.when(ok)
            def _():
                hop(k, s, direction, origin).wait_send()

    def start_copy(device):
        return pltpu.make_async_remote_copy(
            src_ref=start_out,
            dst_ref=start_in,
            send_sem=s_send.at[0],
            recv_sem=s_recv.at[0],
            device_id=device,
            device_id_type=MESH,
        )

    if helped:
        pl.when(is_end)(lambda: start_copy((row, col, helper_of)).start())
    for k in range(n_block):
        loads[k].wait()
        send(k, 0)


    def aligned(index):
        return pl.multiple_of(index, 8)

    class Sum:
        def __init__(self, index, source, target, area, compact=False):
            self.index, self.source, self.target, self.area = index, source, target, area
            self.compact = compact

        def copy(self, src, dst, event, device):
            return pltpu.make_async_remote_copy(
                src_ref=src,
                dst_ref=dst,
                send_sem=p_send.at[self.index, event],
                recv_sem=p_recv.at[self.index, event],
                device_id=device,
                device_id_type=MESH,
            )

        def core_copy(self):
            other = 1 - place["core"]
            return self.copy(
                self.source.at[pl.ds(aligned(other * plan.core), plan.core), :],
                self.area.at[pl.ds(0, plan.core), :],
                0,
                peer("core", other),
            )

        def core_add(self):
            self.core_copy().wait()
            mine = pl.ds(aligned(place["core"] * plan.core), plan.core)
            self.area[pl.ds(plan.core, plan.core), :] = (
                self.source[mine, :] + self.area[pl.ds(0, plan.core), :]
            )

        def step_copies(self, j):
            copies = []
            for path, dims in enumerate(plan.paths):
                n, kind = dims[j]
                size = plan.sizes[path][j]
                base = plan.core + path * plan.length if j == 0 else plan.sums[path][j - 1]
                for p, other in enumerate(others(n, kind)):
                    copies.append(
                        self.copy(
                            self.area.at[pl.ds(aligned(base + other * size), size), :],
                            self.area.at[pl.ds(plan.land[path][j] + p * size, size), :],
                            plan.events[path][j] + p,
                            peer(kind, other),
                        )
                    )
            return copies

        def offset(self, path, j):
            at = place["core"] * plan.core + path * plan.length
            for (_, kind), size in zip(plan.paths[path][:j], plan.sizes[path][:j]):
                at = at + place[kind] * size
            return at

        def step_add(self, j):
            for copy in self.step_copies(j):
                copy.wait()
            for path, dims in enumerate(plan.paths):
                n, kind = dims[j]
                size = plan.sizes[path][j]
                base = plan.core + path * plan.length if j == 0 else plan.sums[path][j - 1]
                total = self.area[pl.ds(aligned(base + place[kind] * size), size), :]
                for p in range(n - 1):
                    total = total + self.area[pl.ds(plan.land[path][j] + p * size, size), :]
                if j + 1 < len(dims):
                    self.area[pl.ds(plan.sums[path][j], size), :] = total
                elif self.compact:
                    self.target[pl.ds(path * plan.shard, size), :] = total
                else:
                    self.target[pl.ds(aligned(self.offset(path, j + 1)), size), :] = total

        def step_back(self, j):
            copies = []
            for path, dims in enumerate(plan.paths):
                n, kind = dims[j]
                size = plan.sizes[path][j]
                mine = pl.ds(aligned(self.offset(path, j + 1)), size)
                for p, other in enumerate(others(n, kind)):
                    copies.append(
                        self.copy(
                            self.target.at[mine, :],
                            self.target.at[mine, :],
                            plan.n_event + plan.events[path][j] + p,
                            peer(kind, other),
                        )
                    )
            return copies

        def core_back(self):
            mine = pl.ds(aligned(place["core"] * plan.core), plan.core)
            return self.copy(
                self.target.at[mine, :],
                self.target.at[mine, :],
                plan.n_event,
                peer("core", 1 - place["core"]),
            )

        def scatter(self, ok=None):
            when(ok, lambda: self.core_copy().start())
            yield
            when(ok, self.core_add)
            for j in range(plan.depth):

                def go(j=j):
                    for copy in self.step_copies(j):
                        copy.start()

                when(ok, go)
                yield
                when(ok, functools.partial(self.step_add, j))

        def gather(self, ok=None):
            for j in reversed(range(plan.depth)):

                def go(j=j):
                    for copy in self.step_back(j):
                        copy.start()

                def land(j=j):
                    for copy in self.step_back(j):
                        copy.wait()

                when(ok, go)
                yield
                when(ok, land)
            when(ok, lambda: self.core_back().start())
            yield
            when(ok, lambda: self.core_back().wait())

    active, summed, finished = [], [], []

    def tick(count=1):
        for _ in range(count):
            for steps in list(active):
                if next(steps, "end") == "end":
                    active.remove(steps)

    def spawn(steps):
        active.append(steps)
        next(steps)


    def find_positions():
        base = (row * n_col + col) * n_grid * rows
        for g in range(n_grid):
            sensor = base + g * rows + lax.broadcasted_iota(jnp.int32, (1, rows), 1)
            positions[g] = 64 * sensor + jitter[g] + 32

    def steer(first_point, count, group, hi_to, lo_to, norm):
        tile = min(32, points)
        tiles = points // tile

        def body(i, carry):
            j, first = i // tiles, pl.multiple_of((i % tiles) * tile, tile)
            pos = positions[group(j)]
            point = first_point() + stride * (
                first + lax.broadcasted_iota(jnp.int32, (tile, 1), 0)
            )
            phase = (point * pos - ((pos & 127) << 15)) << 10
            turns = phase.astype(F32) * F32(2.0**-32)
            value = sine(0.25 - jnp.abs(turns))
            hi, lo = split(value)
            hi_to[j, pl.ds(first, tile), :] = hi
            lo_to[j, pl.ds(first, tile), :] = lo
            if norm:
                part_norm[pl.ds(first, tile), :] += fold(value * value)
            return carry

        lax.fori_loop(0, count * tiles, body, 0)

    def far_group(j):
        return jnp.where(z == 1, z + 1 + j, j)

    def dots(hi, lo, block):
        value = jnp.dot(hi, block, preferred_element_type=F32)
        return value + jnp.dot(lo, block, preferred_element_type=F32)

    def project(k, origin, fresh=False):
        value = dots(steer_hi[origin], steer_lo[origin], held[k, origin])
        if fresh:
            parts[k] = value
        else:
            parts[k] += value

    def project_arrived(k, s, only=None):
        for direction in (0, 1):
            ok, origin = can_receive(s, direction)
            if only is not None:
                ok = jnp.logical_and(ok, only)

            @pl.when(ok)
            def _():
                project(k, origin)

    def project_far(k):
        i = helped.index(k)
        total = None
        for j in range(far_hi.shape[0]):
            value = dots(far_hi[j], far_lo[j], held[k, far_group(j)])
            total = value if total is None else total + value
        far_part[i] = total

    def far_copy(i):
        return pltpu.make_async_remote_copy(
            src_ref=far_sum.at[i],
            dst_ref=far_in.at[i],
            send_sem=f_send.at[i],
            recv_sem=f_recv.at[i],
            device_id=(row, col, end_of),
            device_id_type=MESH,
        )

    sums = [Sum(k, parts.at[k], full.at[k], work.at[k]) for k in range(n_block)]
    norm_sum = Sum(n_block, part_norm, norms, work_norm)
    far_sums = [
        Sum(n_block + 1 + i, far_part.at[i], far_sum.at[i], work.at[n_block + i], compact=True)
        for i in range(len(helped))
    ]

    def add_far(k):
        i = helped.index(k)
        far_copy(i).wait_recv()
        for path in range(len(plan.paths)):
            spot = pl.ds(aligned(sums[k].offset(path, plan.depth)), plan.shard)
            full[k, spot, :] += far_in[i, pl.ds(path * plan.shard, plan.shard), :]

    def reduce(k):
        yield from sums[k].scatter(not_end if k in helped else None)
        yield from sums[k].gather(not_end if k in helped else None)
        summed.append(k)

    def gather_end(k):
        when(is_end, functools.partial(add_far, k))
        yield from sums[k].gather(is_end)

    def reduce_far(k):
        i = helped.index(k)
        yield from far_sums[i].scatter(helps)
        when(helps, lambda: far_copy(i).start())

    def reduce_norm():
        yield from norm_sum.scatter()
        yield from norm_sum.gather()

    def prepare(k):
        value = full[k]
        square = fold(value * value)
        forms[...] = square if k == 0 else forms[...] + square
        hi, lo = split((value / snap).T)
        proj_hi[k] = hi
        proj_lo[k] = lo

    def apply(k):
        def body(g, carry):
            block = held[k, g]
            added = jnp.dot(block, proj_hi[k], preferred_element_type=F32)
            added += jnp.dot(block, proj_lo[k], preferred_element_type=F32)
            spot = pl.ds(pl.multiple_of(g * rows, rows), rows)
            out[spot, :] = added if k == 0 else out[spot, :] + added
            return carry

        lax.fori_loop(0, n_grid, body, 0)

    def finish_block(k, only=None):
        def go():
            prepare(k)
            if k + 1 < n_block:
                apply(k)

        when(only, go)

    codes.wait()
    find_positions()
    part_norm[...] = jnp.zeros_like(part_norm)
    steer(lambda: start_ref[0], n_grid, lambda j: j, steer_hi, steer_lo, True)
    spawn(reduce_norm())
    for k in range(n_block):
        project(k, z, fresh=True)
    tick()
    if helped:

        @pl.when(helps)
        def _():
            start_copy((row, col, end_of)).wait_recv()
            steer(lambda: start_in[0:1, 0:1], n_grid - 2, far_group, far_hi, far_lo, False)

    tick()
    for k in range(n_block):
        receive(k, 0)
        if n_grid > 2:
            send(k, 1, to_end=False)
            if k not in helped:
                send(k, 1, to_end=True)
        project_arrived(k, 0)
        tick()
    early = [sums[k].scatter(is_end) for k in helped]
    for steps in early:
        next(steps)
    for _ in range(plan.depth + 1):
        for steps in early:
            next(steps, None)
    for k in range(n_block):
        if k in helped:
            continue
        for s in range(1, n_grid - 1):
            receive(k, s)
            if s + 1 < n_grid - 1:
                send(k, s + 1)
            project_arrived(k, s)
        spawn(reduce(k))
        tick(2)
    waiting = [(k, s) for k in helped for s in range(1, n_grid - 1)]
    for k in helped:
        spawn(gather_end(k))
        for s in range(1, n_grid - 1):
            receive(k, s, not_end)
            if s + 1 < n_grid - 1:
                send(k, s + 1, to_end=False)
        send(*waiting.pop(0), to_end=True)
        for s in range(1, n_grid - 1):
            project_arrived(k, s, not_end)
        pl.when(helps)(functools.partial(project_far, k))
        spawn(reduce_far(k))
        spawn(reduce(k))
        tick(2)
    tick(2)
    for k, s in waiting:
        send(k, s, to_end=True)
    while active:
        tick()
    for k in range(n_block):
        if k in finished:
            finish_block(k, not_end)
            continue
        if k in helped and k + 1 < n_block:
            for s in range(1, n_grid - 1):
                receive(k, s, is_end)
        finish_block(k)

    outs = [
        pltpu.make_async_copy(src, dst, o_sem.at[i])
        for i, (src, dst) in enumerate(
            (
                (out, partly_ref),
                (proj_hi.at[n_block - 1], hi_ref),
                (proj_lo.at[n_block - 1], lo_ref),
                (forms, forms_ref),
                (norms, norms_ref),
                (held.at[n_block - 1], last_ref),
            )
        )
    ]
    for copy in outs[:-1]:
        copy.start()
    if helped:
        for s in range(1, n_grid - 1):
            receive(n_block - 1, s, is_end)
    outs[-1].start()
    for k in range(n_block):
        for s in range(n_grid - 1):
            drain(k, s)
    if helped:
        pl.when(is_end)(lambda: start_copy((row, col, helper_of)).wait_send())

        @pl.when(helps)
        def _():
            for i in range(len(helped)):
                far_copy(i).wait_send()

    for copy in outs:
        copy.wait()


def finish(snap, partly_ref, held_ref, hi_ref, lo_ref, forms_ref, norms_ref, gamma_ref, noise_ref, out_ref, new_ref):
    block = held_ref[...]
    added = jnp.dot(block, hi_ref[...], preferred_element_type=F32)
    added += jnp.dot(block, lo_ref[...], preferred_element_type=F32)
    out_ref[...] = partly_ref[...] + added

    @pl.when(pl.program_id(0) == 0)
    def _():
        form = jnp.sum(forms_ref[...].T, axis=0, keepdims=True) / snap
        norm = jnp.sum(norms_ref[...].T, axis=0, keepdims=True)
        gamma = gamma_ref[...]
        new_ref[...] = gamma * form / (norm * (gamma + noise_ref[0]))


def on_device(snapshots, jitter_code, slab_start, gamma, noise_var):
    n_row, n_col, n_grid = (lax.axis_size(a) for a in ("row", "col", "grid"))
    rows, snap = snapshots.shape
    group_rows = rows * n_grid
    points = gamma.shape[0]
    width = min(WIDTH, snap)
    n_block = snap // width
    plan = Plan(n_row, n_col, points)
    n_help = len(helped_blocks(n_grid, n_block))
    n_far = max(n_help, 1)
    shard = len(plan.paths) * plan.shard
    vmem = pl.BlockSpec(memory_space=pltpu.VMEM)
    any_space = pl.BlockSpec(memory_space=pl.ANY)
    n_sum = n_block + 1 + n_far
    dma = pltpu.SemaphoreType.DMA
    partly, last, hi, lo, forms, norms = pl.pallas_call(
        functools.partial(kernel, (n_row, n_col, n_grid, GRID // points)),
        out_shape=(
            jax.ShapeDtypeStruct((group_rows, points), F32),
            jax.ShapeDtypeStruct((n_grid, rows, width), BF16),
            jax.ShapeDtypeStruct((width, points), BF16),
            jax.ShapeDtypeStruct((width, points), BF16),
            jax.ShapeDtypeStruct((points, LANES), F32),
            jax.ShapeDtypeStruct((points, LANES), F32),
        ),
        in_specs=[pl.BlockSpec(memory_space=pltpu.SMEM), any_space, any_space],
        out_specs=(any_space,) * 6,
        scratch_shapes=[
            pltpu.VMEM((n_block, n_grid, rows, width), BF16),
            pltpu.VMEM((n_grid, points, rows), BF16),
            pltpu.VMEM((n_grid, points, rows), BF16),
            pltpu.VMEM((max(n_grid - 2, 1), points, rows), BF16),
            pltpu.VMEM((max(n_grid - 2, 1), points, rows), BF16),
            pltpu.VMEM((n_block, points, width), F32),
            pltpu.VMEM((n_far, points, width), F32),
            pltpu.VMEM((n_block, points, width), F32),
            pltpu.VMEM((group_rows, points), F32),
            pltpu.VMEM((n_block, width, points), BF16),
            pltpu.VMEM((n_block, width, points), BF16),
            pltpu.VMEM((points, LANES), F32),
            pltpu.VMEM((points, LANES), F32),
            pltpu.VMEM((points, LANES), F32),
            pltpu.VMEM((n_block + n_far, plan.rows, width), F32),
            pltpu.VMEM((plan.rows, LANES), F32),
            pltpu.VMEM((n_far, shard, width), F32),
            pltpu.VMEM((n_far, shard, width), F32),
            pltpu.VMEM((n_grid, 1, rows), jnp.int32),
            pltpu.VMEM((n_grid, 1, rows), jnp.int32),
            pltpu.VMEM((8, LANES), jnp.int32),
            pltpu.VMEM((8, LANES), jnp.int32),
            dma((n_block,)),
            dma((1,)),
            dma((2, n_block, n_grid - 1)),
            dma((2, n_block, n_grid - 1)),
            dma((n_sum, 2 * plan.n_event)),
            dma((n_sum, 2 * plan.n_event)),
            dma((n_far,)),
            dma((n_far,)),
            dma((1,)),
            dma((1,)),
            dma((6,)),
        ],
        compiler_params=pltpu.CompilerParams(
            collective_id=0, has_side_effects=True, vmem_limit_bytes=34 << 20
        ),
    )(
        slab_start,
        pltpu.with_memory_space_constraint(
            jitter_code.reshape(n_row * n_col, n_grid, 1, rows), pltpu.MemorySpace.HBM
        ),
        pltpu.with_memory_space_constraint(snapshots, pltpu.MemorySpace.HBM),
    )
    tile = min(256, group_rows)

    def whole(*shape):
        return pl.BlockSpec(shape, lambda i: (0, 0))

    def tall(columns):
        return pl.BlockSpec((tile, columns), lambda i: (i, 0))

    steered, gamma_new = pl.pallas_call(
        functools.partial(finish, snap),
        grid=(group_rows // tile,),
        out_shape=(
            jax.ShapeDtypeStruct((group_rows, points), F32),
            jax.ShapeDtypeStruct((1, points), F32),
        ),
        in_specs=[
            tall(points), tall(width), whole(width, points), whole(width, points),
            whole(points, LANES), whole(points, LANES), whole(1, points),
            pl.BlockSpec(memory_space=pltpu.SMEM),
        ],
        out_specs=(tall(points), whole(1, points)),
        compiler_params=pltpu.CompilerParams(vmem_limit_bytes=12 << 20),
    )(
        partly, last.reshape(group_rows, width), hi, lo, forms, norms,
        gamma.reshape(1, points), noise_var,
    )
    return (steered, gamma_new.reshape(points))


def solution(mesh):
    in_specs = (P(("row", "col", "grid"), None), P(), P("grid"), P("grid"), P())
    out_specs = (P(("row", "col"), "grid"), P("grid"))
    return jax.shard_map(
        on_device, mesh=mesh, in_specs=in_specs, out_specs=out_specs, check_vma=False
    )
```

```python
import functools

import jax
import jax.numpy as jnp
from jax import lax
from jax.experimental import pallas as pl
from jax.experimental.pallas import tpu as pltpu
from jax.sharding import PartitionSpec as P

GRID = 65536
WIDTH = 256
LANES = 128
F32 = jnp.float32
BF16 = jnp.bfloat16
MESH = pl.DeviceIdType.MESH


def sine(turns):
    z = turns * turns
    p = F32(39.53581371)
    p = p * z + F32(-76.54965682)
    p = p * z + F32(81.60099819)
    p = p * z + F32(-41.34165493)
    p = p * z + F32(6.28318516)
    return p * turns


def split(x):
    hi = x.astype(BF16)
    return hi, (x - hi.astype(F32)).astype(BF16)


def fold(x):
    n = x.shape[1]
    if n % LANES:
        total = jnp.sum(x, axis=1, keepdims=True)
        lane = lax.broadcasted_iota(jnp.int32, (x.shape[0], LANES), 1)
        return jnp.where(lane == 0, total, 0.0)
    return sum(x[:, a : a + LANES] for a in range(0, n, LANES))


def helped_blocks(n_grid, n_block):
    return list(range(n_block - n_block // 2, n_block)) if n_grid >= 4 else []


class Plan:
    def __init__(self, n_row, n_col, points):
        self.core = points // 2
        rest = [d for d in ((n_col // 2, "y"), (n_row, "row")) if d[0] > 1]
        total = 1
        for n, _ in rest:
            total *= n
        both = len(rest) == 2 and (self.core // total) % 16 == 0
        self.paths = [rest, rest[::-1]] if both else [rest]
        self.length = self.core // len(self.paths)
        self.shard = self.length // total
        self.depth = len(rest)
        at, event = 2 * self.core, 1
        self.land, self.sums, self.events, self.sizes = [], [], [], []
        for dims in self.paths:
            land, sums, events, sizes = [], [], [], []
            size = self.length
            for n, _ in dims:
                size //= n
                land.append(at)
                at += (n - 1) * size
                sums.append(at)
                at += size
                events.append(event)
                event += n - 1
                sizes.append(size)
            self.land.append(land)
            self.sums.append(sums)
            self.events.append(events)
            self.sizes.append(sizes)
        self.rows = at
        self.n_event = event


def kernel(
    sizes, start_ref, jitter_ref, snaps_ref, held_ref, hi_ref, lo_ref, forms_ref, norms_ref,
    held, steer_hi, steer_lo, far_hi, far_lo, parts, far_part, full, proj_hi, proj_lo, forms,
    part_norm, norms, work, work_norm, far_sum, far_in, jitter, positions, start_out, start_in,
    load_sem, misc_sem, z_send, z_recv, p_send, p_recv, f_send, f_recv, s_send, s_recv, o_sem, h_sem,
):
    n_row, n_col, n_grid, stride = sizes
    n_block, _, rows, width = held.shape
    points = parts.shape[1]
    snap = n_block * width
    plan = Plan(n_row, n_col, points)
    helped = helped_blocks(n_grid, n_block)
    row, col, z = (lax.axis_index(a) for a in ("row", "col", "grid"))
    place = {"core": col % 2, "y": col // 2, "row": row}
    is_end = jnp.logical_or(z == 0, z == n_grid - 1)
    not_end = jnp.logical_not(is_end)
    helps = jnp.logical_or(z == 1, z == n_grid - 2)
    if not helped:
        is_end, not_end = None, None
    end_of = jnp.where(z == 1, 0, n_grid - 1)
    helper_of = jnp.where(z == 0, 1, n_grid - 2)

    def when(ok, action):
        if ok is None:
            action()
        else:
            pl.when(ok)(action)

    def peer(kind, other):
        if kind == "row":
            return (other, col, z)
        if kind == "core":
            return (row, (col // 2) * 2 + other, z)
        return (row, other * 2 + col % 2, z)

    def others(n, kind):
        return [lax.rem(place[kind] + p, n) for p in range(1, n)]

    peers = [peer("core", 1 - place["core"])]
    for n, kind in plan.paths[0]:
        peers += [peer(kind, other) for other in others(n, kind)]
    up, down = (row, col, z + 1), (row, col, z - 1)

    loads = [
        pltpu.make_async_copy(
            snaps_ref.at[:, pl.ds(k * width, width)], held.at[k, z], load_sem.at[k]
        )
        for k in range(n_block)
    ]
    for load in loads:
        load.start()
    codes = pltpu.make_async_copy(jitter_ref.at[row * n_col + col], jitter, misc_sem.at[0])
    codes.start()
    start_out[...] = jnp.full(start_out.shape, start_ref[0], jnp.int32)
    barrier = pltpu.get_barrier_semaphore()
    for device in peers:
        pl.semaphore_signal(barrier, inc=1, device_id=device, device_id_type=MESH)

    @pl.when(z + 1 < n_grid)
    def _():
        pl.semaphore_signal(barrier, inc=1, device_id=up, device_id_type=MESH)

    @pl.when(z > 0)
    def _():
        pl.semaphore_signal(barrier, inc=1, device_id=down, device_id_type=MESH)

    beside = jnp.minimum(z, 1) + jnp.minimum(n_grid - 1 - z, 1)
    pl.semaphore_wait(barrier, len(peers) + beside)


    def hop(k, s, direction, origin):
        return pltpu.make_async_remote_copy(
            src_ref=held.at[k, origin],
            dst_ref=held.at[k, origin],
            send_sem=z_send.at[direction, k, s],
            recv_sem=z_recv.at[direction, k, s],
            device_id=up if direction == 0 else down,
            device_id_type=MESH,
        )

    def can_send(s, direction):
        if direction == 0:
            return jnp.logical_and(z + 1 < n_grid, z - s >= 0), z - s
        return jnp.logical_and(z > 0, z + s < n_grid), z + s

    def can_receive(s, direction):
        if direction == 0:
            return z - s - 1 >= 0, z - s - 1
        return z + s + 1 < n_grid, z + s + 1

    def send(k, s, to_end=None):
        for direction in (0, 1):
            ok, origin = can_send(s, direction)
            if to_end is not None:
                last = z + 1 == n_grid - 1 if direction == 0 else z - 1 == 0
                ok = jnp.logical_and(ok, last if to_end else jnp.logical_not(last))

            @pl.when(ok)
            def _():
                hop(k, s, direction, origin).start()

    def keep(k, origin):
        return pltpu.make_async_copy(
            held.at[k, origin], held_ref.at[k, origin], h_sem.at[k, origin]
        )

    def receive(k, s, only=None):
        for direction in (0, 1):
            ok, origin = can_receive(s, direction)
            if only is not None:
                ok = jnp.logical_and(ok, only)

            @pl.when(ok)
            def _():
                hop(k, s, direction, origin).wait_recv()
                keep(k, origin).start()

    def drain(k, s):
        for direction in (0, 1):
            ok, origin = can_send(s, direction)

            @pl.when(ok)
            def _():
                hop(k, s, direction, origin).wait_send()

    def start_copy(device):
        return pltpu.make_async_remote_copy(
            src_ref=start_out,
            dst_ref=start_in,
            send_sem=s_send.at[0],
            recv_sem=s_recv.at[0],
            device_id=device,
            device_id_type=MESH,
        )

    if helped:
        pl.when(is_end)(lambda: start_copy((row, col, helper_of)).start())
    for k in range(n_block):
        loads[k].wait()
        send(k, 0)
        keep(k, z).start()


    def aligned(index):
        return pl.multiple_of(index, 8)

    class Sum:
        def __init__(self, index, source, target, area, compact=False):
            self.index, self.source, self.target, self.area = index, source, target, area
            self.compact = compact

        def copy(self, src, dst, event, device):
            return pltpu.make_async_remote_copy(
                src_ref=src,
                dst_ref=dst,
                send_sem=p_send.at[self.index, event],
                recv_sem=p_recv.at[self.index, event],
                device_id=device,
                device_id_type=MESH,
            )

        def core_copy(self):
            other = 1 - place["core"]
            return self.copy(
                self.source.at[pl.ds(aligned(other * plan.core), plan.core), :],
                self.area.at[pl.ds(0, plan.core), :],
                0,
                peer("core", other),
            )

        def core_add(self):
            self.core_copy().wait()
            mine = pl.ds(aligned(place["core"] * plan.core), plan.core)
            self.area[pl.ds(plan.core, plan.core), :] = (
                self.source[mine, :] + self.area[pl.ds(0, plan.core), :]
            )

        def step_copies(self, j):
            copies = []
            for path, dims in enumerate(plan.paths):
                n, kind = dims[j]
                size = plan.sizes[path][j]
                base = plan.core + path * plan.length if j == 0 else plan.sums[path][j - 1]
                for p, other in enumerate(others(n, kind)):
                    copies.append(
                        self.copy(
                            self.area.at[pl.ds(aligned(base + other * size), size), :],
                            self.area.at[pl.ds(plan.land[path][j] + p * size, size), :],
                            plan.events[path][j] + p,
                            peer(kind, other),
                        )
                    )
            return copies

        def offset(self, path, j):
            at = place["core"] * plan.core + path * plan.length
            for (_, kind), size in zip(plan.paths[path][:j], plan.sizes[path][:j]):
                at = at + place[kind] * size
            return at

        def step_add(self, j):
            for copy in self.step_copies(j):
                copy.wait()
            for path, dims in enumerate(plan.paths):
                n, kind = dims[j]
                size = plan.sizes[path][j]
                base = plan.core + path * plan.length if j == 0 else plan.sums[path][j - 1]
                total = self.area[pl.ds(aligned(base + place[kind] * size), size), :]
                for p in range(n - 1):
                    total = total + self.area[pl.ds(plan.land[path][j] + p * size, size), :]
                if j + 1 < len(dims):
                    self.area[pl.ds(plan.sums[path][j], size), :] = total
                elif self.compact:
                    self.target[pl.ds(path * plan.shard, size), :] = total
                else:
                    self.target[pl.ds(aligned(self.offset(path, j + 1)), size), :] = total

        def step_back(self, j):
            copies = []
            for path, dims in enumerate(plan.paths):
                n, kind = dims[j]
                size = plan.sizes[path][j]
                mine = pl.ds(aligned(self.offset(path, j + 1)), size)
                for p, other in enumerate(others(n, kind)):
                    copies.append(
                        self.copy(
                            self.target.at[mine, :],
                            self.target.at[mine, :],
                            plan.n_event + plan.events[path][j] + p,
                            peer(kind, other),
                        )
                    )
            return copies

        def core_back(self):
            mine = pl.ds(aligned(place["core"] * plan.core), plan.core)
            return self.copy(
                self.target.at[mine, :],
                self.target.at[mine, :],
                plan.n_event,
                peer("core", 1 - place["core"]),
            )

        def scatter(self, ok=None):
            when(ok, lambda: self.core_copy().start())
            yield
            when(ok, self.core_add)
            for j in range(plan.depth):

                def go(j=j):
                    for copy in self.step_copies(j):
                        copy.start()

                when(ok, go)
                yield
                when(ok, functools.partial(self.step_add, j))

        def gather(self, ok=None):
            for j in reversed(range(plan.depth)):

                def go(j=j):
                    for copy in self.step_back(j):
                        copy.start()

                def land(j=j):
                    for copy in self.step_back(j):
                        copy.wait()

                when(ok, go)
                yield
                when(ok, land)
            when(ok, lambda: self.core_back().start())
            yield
            when(ok, lambda: self.core_back().wait())

    active, summed, finished = [], [], []

    def tick(count=1):
        for _ in range(count):
            for steps in list(active):
                if next(steps, "end") == "end":
                    active.remove(steps)

    def spawn(steps):
        active.append(steps)
        next(steps)


    def find_positions():
        base = (row * n_col + col) * n_grid * rows
        for g in range(n_grid):
            sensor = base + g * rows + lax.broadcasted_iota(jnp.int32, (1, rows), 1)
            positions[g] = 64 * sensor + jitter[g] + 32

    def steer(first_point, count, group, hi_to, lo_to, norm):
        tile = min(32, points)
        tiles = points // tile

        def body(i, carry):
            j, first = i // tiles, pl.multiple_of((i % tiles) * tile, tile)
            pos = positions[group(j)]
            point = first_point() + stride * (
                first + lax.broadcasted_iota(jnp.int32, (tile, 1), 0)
            )
            phase = (point * pos - ((pos & 127) << 15)) << 10
            turns = phase.astype(F32) * F32(2.0**-32)
            value = sine(0.25 - jnp.abs(turns))
            hi, lo = split(value)
            hi_to[j, pl.ds(first, tile), :] = hi
            lo_to[j, pl.ds(first, tile), :] = lo
            if norm:
                part_norm[pl.ds(first, tile), :] += fold(value * value)
            return carry

        lax.fori_loop(0, count * tiles, body, 0)

    def far_group(j):
        return jnp.where(z == 1, z + 1 + j, j)

    def dots(hi, lo, block):
        value = jnp.dot(hi, block, preferred_element_type=F32)
        return value + jnp.dot(lo, block, preferred_element_type=F32)

    def project(k, origin, fresh=False):
        value = dots(steer_hi[origin], steer_lo[origin], held[k, origin])
        if fresh:
            parts[k] = value
        else:
            parts[k] += value

    def project_arrived(k, s, only=None):
        for direction in (0, 1):
            ok, origin = can_receive(s, direction)
            if only is not None:
                ok = jnp.logical_and(ok, only)

            @pl.when(ok)
            def _():
                project(k, origin)

    def project_far(k):
        i = helped.index(k)
        total = None
        for j in range(far_hi.shape[0]):
            value = dots(far_hi[j], far_lo[j], held[k, far_group(j)])
            total = value if total is None else total + value
        far_part[i] = total

    def far_copy(i):
        return pltpu.make_async_remote_copy(
            src_ref=far_sum.at[i],
            dst_ref=far_in.at[i],
            send_sem=f_send.at[i],
            recv_sem=f_recv.at[i],
            device_id=(row, col, end_of),
            device_id_type=MESH,
        )

    sums = [Sum(k, parts.at[k], full.at[k], work.at[k]) for k in range(n_block)]
    norm_sum = Sum(n_block, part_norm, norms, work_norm)
    far_sums = [
        Sum(n_block + 1 + i, far_part.at[i], far_sum.at[i], work.at[n_block + i], compact=True)
        for i in range(len(helped))
    ]

    def add_far(k):
        i = helped.index(k)
        far_copy(i).wait_recv()
        for path in range(len(plan.paths)):
            spot = pl.ds(aligned(sums[k].offset(path, plan.depth)), plan.shard)
            full[k, spot, :] += far_in[i, pl.ds(path * plan.shard, plan.shard), :]

    def reduce(k):
        yield from sums[k].scatter(not_end if k in helped else None)
        yield from sums[k].gather(not_end if k in helped else None)
        summed.append(k)

    def gather_end(k):
        when(is_end, functools.partial(add_far, k))
        yield from sums[k].gather(is_end)

    def reduce_far(k):
        i = helped.index(k)
        yield from far_sums[i].scatter(helps)
        when(helps, lambda: far_copy(i).start())

    def reduce_norm():
        yield from norm_sum.scatter()
        yield from norm_sum.gather()

    def kept_projections(k):
        return [
            pltpu.make_async_copy(proj_hi.at[k], hi_ref.at[k], o_sem.at[2 * k]),
            pltpu.make_async_copy(proj_lo.at[k], lo_ref.at[k], o_sem.at[2 * k + 1]),
        ]

    def prepare(k):
        value = full[k]
        square = fold(value * value)
        forms[...] = square if k == 0 else forms[...] + square
        hi, lo = split((value / snap).T)
        proj_hi[k] = hi
        proj_lo[k] = lo
        for copy in kept_projections(k):
            copy.start()

    codes.wait()
    find_positions()
    part_norm[...] = jnp.zeros_like(part_norm)
    steer(lambda: start_ref[0], n_grid, lambda j: j, steer_hi, steer_lo, True)
    spawn(reduce_norm())
    for k in range(n_block):
        project(k, z, fresh=True)
    tick()
    if helped:

        @pl.when(helps)
        def _():
            start_copy((row, col, end_of)).wait_recv()
            steer(lambda: start_in[0:1, 0:1], n_grid - 2, far_group, far_hi, far_lo, False)

    tick()
    for k in range(n_block):
        receive(k, 0)
        if n_grid > 2:
            send(k, 1, to_end=False)
            if k not in helped:
                send(k, 1, to_end=True)
        project_arrived(k, 0)
        tick()
    early = [sums[k].scatter(is_end) for k in helped]
    for steps in early:
        next(steps)
    for _ in range(plan.depth + 1):
        for steps in early:
            next(steps, None)
    for k in range(n_block):
        if k in helped:
            continue
        for s in range(1, n_grid - 1):
            receive(k, s)
            if s + 1 < n_grid - 1:
                send(k, s + 1)
            project_arrived(k, s)
        spawn(reduce(k))
        tick(2)
    waiting = [(k, s) for k in helped for s in range(1, n_grid - 1)]
    for k in helped:
        spawn(gather_end(k))
        for s in range(1, n_grid - 1):
            receive(k, s, not_end)
            if s + 1 < n_grid - 1:
                send(k, s + 1, to_end=False)
        send(*waiting.pop(0), to_end=True)
        for s in range(1, n_grid - 1):
            project_arrived(k, s, not_end)
        pl.when(helps)(functools.partial(project_far, k))
        spawn(reduce_far(k))
        spawn(reduce(k))
        tick(2)
    tick(2)
    for k, s in waiting:
        send(k, s, to_end=True)
    for k in range(n_block):
        if k in summed and k not in helped:
            prepare(k)
            finished.append(k)
    while active:
        tick()
    for k in range(n_block):
        if k not in finished:
            prepare(k)
    outs = [
        pltpu.make_async_copy(src, dst, o_sem.at[2 * n_block + i])
        for i, (src, dst) in enumerate(((forms, forms_ref), (norms, norms_ref)))
    ]
    for copy in outs:
        copy.start()
    for k in helped:
        for s in range(1, n_grid - 1):
            receive(k, s, is_end)
    for k in range(n_block):
        for s in range(n_grid - 1):
            drain(k, s)
    if helped:
        pl.when(is_end)(lambda: start_copy((row, col, helper_of)).wait_send())

        @pl.when(helps)
        def _():
            for i in range(len(helped)):
                far_copy(i).wait_send()

    for k in range(n_block):
        outs += kept_projections(k)
        outs += [keep(k, g) for g in range(n_grid)]
    for copy in outs:
        copy.wait()


def finish(snap, held_ref, hi_ref, lo_ref, forms_ref, norms_ref, gamma_ref, noise_ref, out_ref, new_ref):
    total = None
    for k in range(held_ref.shape[0]):
        added = jnp.dot(held_ref[k], hi_ref[k], preferred_element_type=F32)
        added += jnp.dot(held_ref[k], lo_ref[k], preferred_element_type=F32)
        total = added if total is None else total + added
    out_ref[...] = total

    @pl.when(pl.program_id(0) == 0)
    def _():
        form = jnp.sum(forms_ref[...].T, axis=0, keepdims=True) / snap
        norm = jnp.sum(norms_ref[...].T, axis=0, keepdims=True)
        gamma = gamma_ref[...]
        new_ref[...] = gamma * form / (norm * (gamma + noise_ref[0]))


def on_device(snapshots, jitter_code, slab_start, gamma, noise_var):
    n_row, n_col, n_grid = (lax.axis_size(a) for a in ("row", "col", "grid"))
    rows, snap = snapshots.shape
    group_rows = rows * n_grid
    points = gamma.shape[0]
    width = min(WIDTH, snap)
    n_block = snap // width
    plan = Plan(n_row, n_col, points)
    n_help = len(helped_blocks(n_grid, n_block))
    n_far = max(n_help, 1)
    shard = len(plan.paths) * plan.shard
    vmem = pl.BlockSpec(memory_space=pltpu.VMEM)
    any_space = pl.BlockSpec(memory_space=pl.ANY)
    n_sum = n_block + 1 + n_far
    dma = pltpu.SemaphoreType.DMA
    held, hi, lo, forms, norms = pl.pallas_call(
        functools.partial(kernel, (n_row, n_col, n_grid, GRID // points)),
        out_shape=(
            jax.ShapeDtypeStruct((n_block, n_grid, rows, width), BF16),
            jax.ShapeDtypeStruct((n_block, width, points), BF16),
            jax.ShapeDtypeStruct((n_block, width, points), BF16),
            jax.ShapeDtypeStruct((points, LANES), F32),
            jax.ShapeDtypeStruct((points, LANES), F32),
        ),
        in_specs=[pl.BlockSpec(memory_space=pltpu.SMEM), any_space, any_space],
        out_specs=(any_space,) * 5,
        scratch_shapes=[
            pltpu.VMEM((n_block, n_grid, rows, width), BF16),
            pltpu.VMEM((n_grid, points, rows), BF16),
            pltpu.VMEM((n_grid, points, rows), BF16),
            pltpu.VMEM((max(n_grid - 2, 1), points, rows), BF16),
            pltpu.VMEM((max(n_grid - 2, 1), points, rows), BF16),
            pltpu.VMEM((n_block, points, width), F32),
            pltpu.VMEM((n_far, points, width), F32),
            pltpu.VMEM((n_block, points, width), F32),
            pltpu.VMEM((n_block, width, points), BF16),
            pltpu.VMEM((n_block, width, points), BF16),
            pltpu.VMEM((points, LANES), F32),
            pltpu.VMEM((points, LANES), F32),
            pltpu.VMEM((points, LANES), F32),
            pltpu.VMEM((n_block + n_far, plan.rows, width), F32),
            pltpu.VMEM((plan.rows, LANES), F32),
            pltpu.VMEM((n_far, shard, width), F32),
            pltpu.VMEM((n_far, shard, width), F32),
            pltpu.VMEM((n_grid, 1, rows), jnp.int32),
            pltpu.VMEM((n_grid, 1, rows), jnp.int32),
            pltpu.VMEM((8, LANES), jnp.int32),
            pltpu.VMEM((8, LANES), jnp.int32),
            dma((n_block,)),
            dma((1,)),
            dma((2, n_block, n_grid - 1)),
            dma((2, n_block, n_grid - 1)),
            dma((n_sum, 2 * plan.n_event)),
            dma((n_sum, 2 * plan.n_event)),
            dma((n_far,)),
            dma((n_far,)),
            dma((1,)),
            dma((1,)),
            dma((2 * n_block + 2,)),
            dma((n_block, n_grid)),
        ],
        compiler_params=pltpu.CompilerParams(
            collective_id=0, has_side_effects=True, vmem_limit_bytes=32 << 20
        ),
    )(
        slab_start,
        pltpu.with_memory_space_constraint(
            jitter_code.reshape(n_row * n_col, n_grid, 1, rows), pltpu.MemorySpace.HBM
        ),
        pltpu.with_memory_space_constraint(snapshots, pltpu.MemorySpace.HBM),
    )
    tile = min(256, group_rows)

    def whole(*shape):
        return pl.BlockSpec(shape, lambda i: (0, 0))

    def tall(columns):
        return pl.BlockSpec((tile, columns), lambda i: (i, 0))

    steered, gamma_new = pl.pallas_call(
        functools.partial(finish, snap),
        grid=(group_rows // tile,),
        out_shape=(
            jax.ShapeDtypeStruct((group_rows, points), F32),
            jax.ShapeDtypeStruct((1, points), F32),
        ),
        in_specs=[
            pl.BlockSpec((n_block, tile, width), lambda i: (0, i, 0)),
            pl.BlockSpec((n_block, width, points), lambda i: (0, 0, 0)),
            pl.BlockSpec((n_block, width, points), lambda i: (0, 0, 0)),
            whole(points, LANES), whole(points, LANES), whole(1, points),
            pl.BlockSpec(memory_space=pltpu.SMEM),
        ],
        out_specs=(tall(points), whole(1, points)),
        compiler_params=pltpu.CompilerParams(vmem_limit_bytes=12 << 20),
    )(
        held.reshape(n_block, group_rows, width), hi, lo, forms, norms,
        gamma.reshape(1, points), noise_var,
    )
    return (steered, gamma_new.reshape(points))


def solution(mesh):
    in_specs = (P(("row", "col", "grid"), None), P(), P("grid"), P("grid"), P())
    out_specs = (P(("row", "col"), "grid"), P("grid"))
    return jax.shard_map(
        on_device, mesh=mesh, in_specs=in_specs, out_specs=out_specs, check_vma=False
    )
```
